256 devices in a mesh: seq: 16 (over z, core), pipe: 4 (over y), dp: 4 (over x).
Axes of the slice: x: 4, y: 4, z: 8, core: 2. Of those that a mesh axis runs over, the one named last changes fastest.
Arguments:
- segment_input: bfloat16 [4, 4096, 3072], P('pipe', ('dp', 'seq')), parts along dimension 1
- output_grad: bfloat16 [4, 4096, 3072], P('pipe', ('dp', 'seq')), parts along dimension 1, may hold values from -6 to 6
- qkv_weight: bfloat16 [4, 3072, 16, 384], P('pipe', None, 'seq')
- out_weight: bfloat16 [4, 2048, 3072], P('pipe', 'seq'), may hold values from -0.125 to 0.125
- query_gain: float32 [4, 128], P('pipe')
- key_gain: float32 [4, 128], P('pipe')
- gate_scale: float32 [4, 3072], P('pipe'), may hold values from -4 to 4
- neighbours: int32 [64, 27], P('dp'), parts along dimension 0, may hold values from -1 to 15, as said below
- tile_slot: int32 [64], P('dp'), parts along dimension 0, may hold values from 0 to 15, as said below
Outputs:
- segment_output: bfloat16 [4, 4096, 3072], P('pipe', ('dp', 'seq')), parts along dimension 1
- input_grad: bfloat16 [4, 4096, 3072], P('pipe', ('dp', 'seq')), parts along dimension 1
- gate_grad: float32 [16, 3072], P(('dp', 'pipe'), 'seq'), parts along dimension 0
The draws below stay inside these ranges and needn't reach their ends.
There are 4 independent parts, one for each index of `dp`. The reference program is written for one: setup_inputs(seed, part) draws one part's arguments, and reference() takes and returns one part's arrays. A program takes and returns all parts, laid end to end along the dimension named above; an argument that names none is the same for every part. Nothing has to cross between parts.
Inputs may be any that keep to these rules, and one draw needn't show every extreme that they name: `neighbours`: row t lists tile t and every tile whose position in the clip's 3-D grid of tiles differs from t's by at most one along each of the three dimensions, one fixed place for each of the 27 offsets, with -1 where an offset leaves the grid; if u lists t then t lists u. `tile_slot`: A permutation of 0 to 15.
All inputs are finite; a program needn't handle non-finite values.
Results may differ from the reference program's by a relative error of at most 0.02.
Values may be sent and summed in bfloat16 or wider, within the bound.
A program may use at most 128 MiB of HBM per device.

```python
import math
import jax
import jax.numpy as jnp
from jax import lax

D = 3072
HD = 128
HEADS = 16
TILE = 64
NB = 27
SECTIONS = 4
HEAD_DEV = 1
TILES = 16
TOKENS = 1024
N_SEQ = 16


def grid_shape(tile_count):
    shape_dims = [1, 1, 1]
    remaining = tile_count
    factor = 2
    while remaining > 1:
        if remaining % factor == 0:
            shape_dims.sort()
            shape_dims[0] = shape_dims[0] * factor
            remaining = remaining // factor
        else:
            factor = factor + 1
    shape_dims.sort()
    return shape_dims


def tile_layout(key):
    relabel = jax.random.permutation(jax.random.fold_in(key, 11), TILES).astype(jnp.int32)
    grid_dims = grid_shape(TILES)
    depth = grid_dims[0]
    height = grid_dims[1]
    breadth = grid_dims[2]
    raster = jnp.arange(TILES, dtype=jnp.int32)
    along_depth = raster // (height * breadth)
    along_height = raster // breadth % height
    along_breadth = raster % breadth
    columns = []
    for step_depth in (-1, 0, 1):
        for step_height in (-1, 0, 1):
            for step_breadth in (-1, 0, 1):
                moved_depth = along_depth + step_depth
                moved_height = along_height + step_height
                moved_breadth = along_breadth + step_breadth
                inside = (moved_depth >= 0) & (moved_depth < depth) & (moved_height >= 0) & (moved_height < height) & (moved_breadth >= 0) & (moved_breadth < breadth)
                target = jnp.clip(moved_depth * height * breadth + moved_height * breadth + moved_breadth, 0, TILES - 1)
                columns.append(jnp.where(inside, relabel[target], -1))
    listed_rows = jnp.stack(columns, axis=1).astype(jnp.int32)
    neighbour_table = jnp.zeros((TILES, NB), jnp.int32).at[relabel].set(listed_rows)
    slot_table = jnp.zeros((TILES,), jnp.int32).at[relabel].set(raster)
    return (neighbour_table, slot_table)


def draw_neighbours(key, part):
    return tile_layout(key)[0]


def draw_tile_slot(key, part):
    return tile_layout(key)[1]


def draw_segment_input(key, part):
    base_key = jax.random.fold_in(key, 1)
    noise_key = jax.random.fold_in(base_key, 21)
    row_key = jax.random.fold_in(base_key, 22)
    column_key = jax.random.fold_in(base_key, 23)
    full_shape = (SECTIONS, TOKENS, D)
    row_scale = jnp.exp(jax.random.uniform(row_key, (SECTIONS, TOKENS, 1), jnp.float32, math.log(0.3), math.log(3.0)))
    column_scale = jnp.exp(jax.random.uniform(column_key, (1, 1, D), jnp.float32, math.log(0.3), math.log(3.0)))
    values = jax.random.normal(noise_key, full_shape, jnp.float32) * row_scale * column_scale
    return jnp.clip(values, -32.0, 32.0).astype(jnp.bfloat16)


def draw_qkv_weight(key, part):
    base_key = jax.random.fold_in(key, 31)
    part_shape = (SECTIONS, D, HEADS, HD)
    spread = 1.0 / math.sqrt(D)
    value_part = jnp.clip(jax.random.normal(jax.random.fold_in(base_key, 3), part_shape, jnp.float32), -4.0, 4.0) * spread
    query_noise = jnp.clip(jax.random.normal(jax.random.fold_in(base_key, 1), part_shape, jnp.float32), -4.0, 4.0) * spread
    query_part = query_noise
    key_part = jnp.clip(jax.random.normal(jax.random.fold_in(base_key, 2), part_shape, jnp.float32), -4.0, 4.0) * spread
    return jnp.concatenate([query_part, key_part, value_part], axis=-1).astype(jnp.bfloat16)


def gain_pair(key):
    base_key = jax.random.fold_in(key, 5)
    first = jnp.clip(jax.random.normal(jax.random.fold_in(base_key, 1), (SECTIONS, HD), jnp.float32), -3.5, 3.5)
    second = jnp.clip(jax.random.normal(jax.random.fold_in(base_key, 2), (SECTIONS, HD), jnp.float32), -3.5, 3.5)
    return (first, second)


def draw_query_gain(key, part):
    return gain_pair(key)[0]


def draw_key_gain(key, part):
    return gain_pair(key)[1]


def block_scale(rng, shape, pieces, least, high):
    def one(dim, blocks):
        draws = jax.random.uniform(jax.random.fold_in(jax.random.fold_in(rng, 6), dim), (blocks,), jnp.float32, least / len(pieces), high / len(pieces))
        return jnp.repeat(jnp.exp(draws), shape[dim] // blocks).reshape((-1,) + (1,) * (len(shape) - dim - 1))

    level = one(*pieces[0])
    for cut in pieces[1:]:
        level = level * one(*cut)
    return level


def scatter_about(own_key, shape, scale, reach, pieces=(), held_as=jnp.bfloat16):
    entries = scale * jax.random.normal(own_key, shape, jnp.float32)
    if pieces:
        entries = entries * block_scale(own_key, shape, pieces, -0.22, 0.18)
    return jnp.clip(entries, -reach, reach).astype(held_as)


def setup_inputs(seed: int = 0, part: int = 0) -> dict:
    splits = jax.random.split(jax.random.key(seed), 10)
    part_splits = jax.random.split(jax.random.fold_in(splits[9], part), 10)
    return {
        "segment_input": draw_segment_input(jax.random.fold_in(jax.random.fold_in(splits[9], part), 71), part),
        "output_grad": scatter_about(part_splits[1], (SECTIONS, TOKENS, D), 1.0, 6.0, ((0, 4), (1, 16))),
        "qkv_weight": draw_qkv_weight(jax.random.fold_in(splits[9], 71), part),
        "out_weight": scatter_about(splits[3], (SECTIONS, HEADS * HD, D), (HEADS * HD) ** -0.5, 0.125, ((0, 4), (1, 16))),
        "query_gain": draw_query_gain(jax.random.fold_in(splits[9], 71), part),
        "key_gain": draw_key_gain(jax.random.fold_in(splits[9], 71), part),
        "gate_scale": scatter_about(splits[6], (SECTIONS, D), 1.0, 4.0, ((0, 4),), jnp.float32),
        "neighbours": draw_neighbours(jax.random.fold_in(jax.random.fold_in(splits[9], part), 71), part),
        "tile_slot": draw_tile_slot(jax.random.fold_in(jax.random.fold_in(splits[9], part), 71), part),
    }


EPSILON = 1e-06

def slot_lists(neighbours, tile_slot):
    tile_count = tile_slot.shape[0]
    numbering = jnp.arange(tile_count, dtype=jnp.int32)
    tile_of_slot = jnp.zeros((tile_count,), jnp.int32).at[tile_slot].set(numbering)
    listed_tiles = neighbours[tile_of_slot]
    key_valid = listed_tiles >= 0
    key_slots = jnp.where(key_valid, tile_slot[jnp.maximum(listed_tiles, 0)], 0).astype(jnp.int32)
    return (key_slots, key_valid)

def unit_norm(values):
    spread = jnp.sqrt(lax.optimization_barrier(jnp.mean(values * values, axis=-1, keepdims=True)) + EPSILON)
    return (values / spread, spread)

def block_tiles():
    return math.gcd(TILES, max(1, 512 // TILE))

def probabilities(query_block, key_rows, block_valid):
    scores = jnp.einsum('aihd,ajhd->ahij', query_block.astype(jnp.float32), key_rows.astype(jnp.float32)) * (1.0 / math.sqrt(HD))
    key_mask = jnp.repeat(block_valid, TILE, axis=1)
    scores = jnp.where(key_mask[:, None, None, :], scores, -jnp.inf)
    row_max = lax.optimization_barrier(jnp.max(scores, axis=-1, keepdims=True))
    weights = jnp.exp(scores - row_max)
    return (weights / lax.optimization_barrier(jnp.sum(weights, axis=-1, keepdims=True))).astype(jnp.bfloat16)

def gathered(tiles_array, block_slots):
    return tiles_array[block_slots].reshape(block_slots.shape[0], NB * TILE, HEADS, HD)

def attend_both(queries, keys_normed, value_rows_all, attended_grad, key_slots, key_valid):
    query_tiles = queries.reshape(TILES, TILE, HEADS, HD)
    key_tiles = keys_normed.reshape(TILES, TILE, HEADS, HD)
    value_tiles = value_rows_all.reshape(TILES, TILE, HEADS, HD)
    grad_tiles = attended_grad.reshape(TILES, TILE, HEADS, HD)
    span = block_tiles()
    scale_factor = 1.0 / math.sqrt(HD)
    empty_grad = jnp.zeros((TILES, TILE, HEADS, HD), jnp.float32)

    def per_block(accumulators, block_index):
        key_total, value_total = accumulators
        first_tile = block_index * span
        query_block = lax.dynamic_slice_in_dim(query_tiles, first_tile, span, 0)
        grad_block = lax.dynamic_slice_in_dim(grad_tiles, first_tile, span, 0).astype(jnp.float32)
        block_slots = lax.dynamic_slice_in_dim(key_slots, first_tile, span, 0)
        block_valid = lax.dynamic_slice_in_dim(key_valid, first_tile, span, 0)
        key_rows = gathered(key_tiles, block_slots).astype(jnp.float32)
        value_rows = gathered(value_tiles, block_slots).astype(jnp.float32)
        weights_wide = probabilities(query_block, key_rows, block_valid).astype(jnp.float32)
        attended = jnp.einsum('ahij,ajhd->aihd', weights_wide, value_rows)
        value_part = jnp.einsum('ahij,aihd->ajhd', weights_wide, grad_block)
        prob_grad = jnp.einsum('aihd,ajhd->ahij', grad_block, value_rows)
        row_delta = lax.optimization_barrier(jnp.sum(weights_wide * prob_grad, axis=-1, keepdims=True))
        score_grad = (weights_wide * (prob_grad - row_delta) * scale_factor).astype(jnp.bfloat16)
        score_wide = score_grad.astype(jnp.float32)
        query_part = jnp.einsum('ahij,ajhd->aihd', score_wide, key_rows)
        key_part = jnp.einsum('ahij,aihd->ajhd', score_wide, query_block.astype(jnp.float32))
        block_shape = (span, NB, TILE, HEADS, HD)
        key_total = key_total.at[block_slots].add(key_part.reshape(block_shape))
        value_total = value_total.at[block_slots].add(value_part.reshape(block_shape))
        return ((key_total, value_total), (attended, query_part))
    totals, parts = lax.scan(per_block, (empty_grad, empty_grad), jnp.arange(TILES // span, dtype=jnp.int32))
    flat_shape = (TOKENS, HEADS, HD)
    return (parts[0].reshape(flat_shape), parts[1].reshape(flat_shape), totals[0].reshape(flat_shape), totals[1].reshape(flat_shape))

def section(stream, upstream, weight_in, weight_out, query_weights, key_weights, gate_weights, key_slots, key_valid):
    weight_flat = weight_in.reshape(D, HEADS * 3 * HD)
    projected = jnp.dot(stream, weight_flat, preferred_element_type=jnp.float32).reshape(TOKENS, HEADS, 3, HD)
    query_unit, query_spread = unit_norm(projected[:, :, 0])
    key_unit, key_spread = unit_norm(projected[:, :, 1])
    queries = (query_unit * query_weights).astype(jnp.bfloat16)
    keys_normed = (key_unit * key_weights).astype(jnp.bfloat16)
    value_rows = projected[:, :, 2].astype(jnp.bfloat16)
    scaled = (upstream.astype(jnp.float32) * gate_weights).astype(jnp.bfloat16)
    attended_grad = jnp.dot(scaled, weight_out.T, preferred_element_type=jnp.float32).astype(jnp.bfloat16)
    attended, query_grad, key_grad, value_grad = attend_both(queries, keys_normed, value_rows, attended_grad, key_slots, key_valid)
    attended_low = attended.astype(jnp.bfloat16).reshape(TOKENS, HEADS * HD)
    attention_out = jnp.dot(attended_low, weight_out, preferred_element_type=jnp.float32)
    forward = (stream.astype(jnp.float32) + gate_weights * attention_out).astype(jnp.bfloat16)
    gate_part = lax.optimization_barrier(jnp.sum(upstream.astype(jnp.float32) * attention_out, axis=0))
    query_scaled = query_grad * query_weights
    query_part_grad = (query_scaled - query_unit * lax.optimization_barrier(jnp.mean(query_scaled * query_unit, axis=-1, keepdims=True))) / query_spread
    key_scaled = key_grad * key_weights
    key_part_grad = (key_scaled - key_unit * lax.optimization_barrier(jnp.mean(key_scaled * key_unit, axis=-1, keepdims=True))) / key_spread
    projected_grad = jnp.stack([query_part_grad, key_part_grad, value_grad], axis=2).astype(jnp.bfloat16)
    grouped_grad = projected_grad.reshape(TOKENS, N_SEQ, HEAD_DEV * 3 * HD).astype(jnp.float32)
    grouped_weight = weight_flat.reshape(D, N_SEQ, HEAD_DEV * 3 * HD).astype(jnp.float32)
    group_terms = jnp.einsum('tgc,dgc->gtd', grouped_grad, grouped_weight).astype(jnp.bfloat16)
    stream_grad = lax.optimization_barrier(jnp.sum(group_terms.astype(jnp.float32), axis=0))
    backward = (upstream.astype(jnp.float32) + stream_grad).astype(jnp.bfloat16)
    return (forward, backward, gate_part)

def reference(segment_input, output_grad, qkv_weight, out_weight, query_gain, key_gain, gate_scale, neighbours, tile_slot):
    key_slots, key_valid = slot_lists(neighbours, tile_slot)
    forward_parts = []
    gradient_parts = []
    gate_parts = []
    for index in range(SECTIONS):
        result = section(segment_input[index], output_grad[index], qkv_weight[index], out_weight[index], query_gain[index], key_gain[index], gate_scale[index], key_slots, key_valid)
        forward_parts.append(result[0])
        gradient_parts.append(result[1])
        gate_parts.append(result[2])
    segment_output = jnp.roll(jnp.stack(forward_parts), 1, axis=0)
    input_grad = jnp.roll(jnp.stack(gradient_parts), -1, axis=0)
    gate_grad = jnp.stack(gate_parts)
    return (segment_output, input_grad, gate_grad)
```

```python
import functools
import math

import jax
import jax.numpy as jnp
from jax import lax
from jax.experimental import pallas as pl
from jax.experimental.pallas import tpu as pltpu
from jax.sharding import PartitionSpec as P

EPSILON = 1e-06
MESH = pl.DeviceIdType.MESH
F32 = jnp.float32
BF16 = jnp.bfloat16
D = 3072
HD = 128
TILE = 64
NZ = 8
COLS = 512
NT = (((1,), (1,)), ((), ()))


def dot(a, b):
    return jnp.dot(a, b, preferred_element_type=F32)


def dot_nt(a, b):
    return lax.dot_general(a, b, NT, preferred_element_type=F32)


def kernel(
    stream, upstream, wqkv, wout, qgain, kgain, gate, neigh, tslot,
    fwd_out, bwd_out, gate_out,
    Sg, UP, SC, WQ, WO, PJX, PJ1, BIAS, Qb, Kb, Vb, KT, VT, Pb, ATT, AH, DOS, DO,
    dQ, dK, dV, PGO, PGX, PGP, GT, SB, RB, AOUT, AOX, FO, BO, GS, GR,
    ld, zs_s, zs_r, zw_s, zw_r, xw_s, xw_r, pj_s, pj_r, ex_s, ex_r,
    at_s, at_r, do_s, do_r, rs_s, rs_r, y_s, y_r, g_s, g_r,
):
    seq = lax.axis_index("seq")
    x = lax.axis_index("dp")
    y = lax.axis_index("pipe")
    z = lax.div(seq, 2)
    c = lax.rem(seq, 2)

    def dev(d, e=0):
        return {"seq": 2 * lax.rem(z + d, NZ) + (c if e == 0 else 1 - c)}

    right, left, partner = dev(1), dev(NZ - 1), dev(0, 1)
    xr = {"dp": lax.rem(x + 1, 4)}
    xl = {"dp": lax.rem(x + 3, 4)}
    yn = {"pipe": lax.rem(y + 1, 4)}
    yp = {"pipe": lax.rem(y + 3, 4)}

    sent = []

    def remote(src, dst, ssem, rsem, to):
        return pltpu.make_async_remote_copy(
            src_ref=src, dst_ref=dst, send_sem=ssem, recv_sem=rsem,
            device_id=to, device_id_type=MESH)

    def go(copy):
        copy.start()
        sent.append(copy)

    loads = [
        pltpu.make_async_copy(wout, WO.at[0], ld.at[0]),
        pltpu.make_async_copy(stream, Sg.at[0], ld.at[1]),
        pltpu.make_async_copy(upstream, UP.at[0], ld.at[2]),
        pltpu.make_async_copy(wqkv, WQ.at[0], ld.at[3]),
    ]
    for copy in loads:
        copy.start()

    barrier = pltpu.get_barrier_semaphore()
    peers = [dev(d, e) for d in range(NZ) for e in range(2) if d or e] + [xr, xl, yn, yp]
    for peer in peers:
        pl.semaphore_signal(barrier, inc=1, device_id=peer, device_id_type=MESH)
    pl.semaphore_wait(barrier, len(peers))

    def at(way, j):
        return (NZ - j) % NZ if way == 0 else j % NZ

    def ring_to(way):
        return right if way == 0 else left

    def s_unit(way, k):
        j, half = k // 2, (k + way) % 2
        return remote(Sg.at[at(way, j), half], Sg.at[at(way, j + 1), half],
                      zs_s.at[way, k], zs_r.at[way, k], ring_to(way))

    def w_unit(way, m):
        src, dst = WO.at[at(way, m), x], WO.at[at(way, m + 1), x]
        if m == 3:
            src, dst = src.at[way], dst.at[way]
        return remote(src, dst, zw_s.at[way, m], zw_r.at[way, m], ring_to(way))

    def x_unit(d, kind):
        quarter = [x, x, lax.rem(x + 3, 4), lax.rem(x + 1, 4)][kind]
        ref = WO.at[d, quarter]
        if kind >= 2:
            ref = ref.at[kind - 2]
        return remote(ref, ref, xw_s.at[d, kind], xw_r.at[d, kind], xr if kind % 2 == 0 else xl)

    def s_wait(k):
        for way in (0, 1):
            s_unit(way, k).wait_recv()

    def s_next(k):
        s_wait(k)
        if k + 2 <= 6:
            for way in (0, 1):
                go(s_unit(way, k + 2))

    def w_next(m):
        for way in (0, 1):
            w_unit(way, m).wait_recv()
            if m + 1 <= 3:
                go(w_unit(way, m + 1))

    def x_send(d):
        go(x_unit(d, 0))
        go(x_unit(d, 1))

    def x_next(d):
        x_unit(d, 0).wait_recv()
        go(x_unit(d, 2))
        x_unit(d, 1).wait_recv()
        go(x_unit(d, 3))

    def x_done(d):
        x_unit(d, 2).wait_recv()
        x_unit(d, 3).wait_recv()

    def project(ds):
        rows = [Sg.at[d] for d in ds]

        def one(e, carry):
            lhs = [r[...].reshape(TILE, D) for r in rows]
            lhs = lhs[0] if len(lhs) == 1 else jnp.concatenate(lhs, axis=0)
            out = dot(lhs, WQ[e])
            for n, d in enumerate(ds):
                PJX[e, d] = out[n * TILE:(n + 1) * TILE]
            return carry

        lax.fori_loop(0, 2, one, 0)
        for d in ds:
            go(pj_unit(d))

    def pj_unit(d):
        return remote(PJX.at[1, d], PJ1.at[d], pj_s.at[d], pj_r.at[d], partner)

    def do_unit(d):
        return remote(DOS.at[d], DO.at[(NZ - d) % NZ], do_s.at[d], do_r.at[d], dev(d))

    def grads_in(ds):
        for d in ds:
            val = dot_nt(SC[...], WO[d].reshape(HD, D)).astype(BF16)
            if d == 0:
                DO[0] = val
            else:
                DOS[d] = val
                go(do_unit(d))

    up_x = remote(UP.at[0], UP.at[1], ex_s.at[0], ex_r.at[0], partner)
    wq_x = remote(WQ.at[0], WQ.at[1], ex_s.at[1], ex_r.at[1], partner)

    loads[0].wait()
    go(w_unit(0, 0))
    go(w_unit(1, 0))
    loads[1].wait()
    for k in (0, 1):
        for way in (0, 1):
            go(s_unit(way, k))
    loads[2].wait()
    go(up_x)
    loads[3].wait()
    go(wq_x)

    i_rows = lax.broadcasted_iota(jnp.int32, (16, 16), 0)
    rel_z = z + lax.div(i_rows, 2)
    rel_z = jnp.where(rel_z >= NZ, rel_z - NZ, rel_z)
    odd = lax.rem(i_rows, 2)
    rel_slot = 2 * rel_z + jnp.where(odd == 0, c, 1 - c)
    lanes16 = lax.broadcasted_iota(jnp.int32, (16, 16), 1)
    listed = jnp.zeros((16, 16), F32)
    for k in range(neigh.shape[1]):
        listed = listed + jnp.where(neigh[:, k:k + 1] == lanes16, 1.0, 0.0)
    holds = jnp.where(rel_slot == tslot[...], 1.0, 0.0)
    by_key = dot_nt(holds, listed)
    by_key = dot_nt(by_key, holds)
    spread = jnp.where(
        lax.div(lax.broadcasted_iota(jnp.int32, (16, 1024), 1), TILE)
        == lax.broadcasted_iota(jnp.int32, (16, 1024), 0), 1.0, 0.0)
    bias = jnp.where(dot(by_key, spread) > 0.5, 0.0, -jnp.inf)
    for d in range(NZ):
        BIAS[d] = bias[:, d * HD:(d + 1) * HD]

    w_next(0)
    x_send(7)
    x_send(1)
    up_x.wait_recv()
    SC[...] = (UP[...].astype(F32) * gate[...]).astype(BF16).reshape(2 * TILE, D)
    wq_x.wait_recv()
    project([0])
    s_next(0)
    x_next(7)
    s_next(1)
    grads_in([0])
    x_next(1)
    project([7, 1])
    w_next(1)
    x_send(6)
    x_send(2)
    s_next(2)
    x_next(6)
    x_done(7)
    x_done(1)
    grads_in([7, 1])
    s_next(3)
    x_next(2)
    project([6, 2])
    w_next(2)
    x_send(5)
    x_send(3)
    s_next(4)
    x_next(5)
    x_done(6)
    x_done(2)
    grads_in([6, 2])
    s_next(5)
    x_next(3)
    project([5, 3])
    w_next(3)
    x_send(4)
    s_next(6)
    project([4])
    x_done(5)
    x_done(3)
    grads_in([5, 3])
    x_next(4)

    for d in range(NZ):
        pj_unit(d).wait_recv()

    def both(d):
        return jnp.concatenate([PJX[0, d], PJ1[d]], axis=0)

    def unit_of(part):
        spread = jnp.sqrt(jnp.mean(part * part, axis=-1, keepdims=True) + EPSILON)
        return part / spread, spread

    def norm(d, carry):
        pj = both(d)
        q_unit, _ = unit_of(pj[:, :HD])
        k_unit, _ = unit_of(pj[:, HD:2 * HD])
        Qb[d] = (q_unit * qgain[...]).astype(BF16)
        k = k_unit * kgain[...]
        v = pj[:, 2 * HD:]
        Kb[d] = k.astype(BF16)
        Vb[d] = v.astype(BF16)
        cols = pl.ds(pl.multiple_of(d * HD, HD), HD)
        KT[:, cols] = k.T.astype(BF16)
        VT[:, cols] = v.T.astype(BF16)
        return carry

    lax.fori_loop(0, NZ, norm, 0)
    scale = 1.0 / math.sqrt(HD)

    def attend(d, carry):
        s = dot_nt(Kb[...].reshape(NZ * HD, HD), Qb[d]) * scale
        s = s.reshape(16, TILE, HD) + BIAS[d][:, None, :]
        s = s.reshape(NZ * HD, HD)
        p = jnp.exp(s - jnp.max(s, axis=0, keepdims=True))
        p = (p * (1.0 / jnp.sum(p, axis=0, keepdims=True))).astype(BF16)
        Pb[d] = p
        ATT[d] = dot(VT[...], p).T.astype(BF16)
        return carry

    lax.fori_loop(0, NZ, attend, 0)

    def at_unit(d):
        back = (NZ - d) % NZ
        return remote(ATT.at[d], AH.at[:, back * HD:(back + 1) * HD], at_s.at[d], at_r.at[d], dev(d))

    x_done(4)
    grads_in([4])
    for d in range(1, NZ):
        go(at_unit(d))
    AH[:, :HD] = ATT[0]
    dK[...] = jnp.zeros_like(dK)
    dV[...] = jnp.zeros_like(dV)
    for d in range(1, NZ):
        do_unit(d).wait_recv()

    def attend_back(d, carry):
        grad, p = DO[d], Pb[d]
        dV[...] += dot(p, grad)
        dp = dot_nt(Vb[...].reshape(NZ * HD, HD), grad)
        wide = p.astype(F32)
        delta = jnp.sum(wide * dp, axis=0, keepdims=True)
        ds = (wide * (dp - delta) * scale).astype(BF16)
        dK[...] += dot(ds, Qb[d])
        dQ[d] = dot(KT[...], ds).T
        return carry

    lax.fori_loop(0, NZ, attend_back, 0)

    def norm_back(d, carry):
        pj = both(d)
        rows = pl.ds(pl.multiple_of(d * HD, HD), HD)

        def one(part, grad, gain):
            unit, spread = unit_of(part)
            a = grad * gain
            return (a - unit * jnp.mean(a * unit, axis=-1, keepdims=True)) / spread

        gq = one(pj[:, :HD], dQ[d], qgain[...])
        gk = one(pj[:, HD:2 * HD], dK[rows, :], kgain[...])
        pg = jnp.concatenate([gq, gk, dV[rows, :]], axis=1).astype(BF16)
        PGO[d] = pg[:TILE]
        PGX[d] = pg[TILE:]
        return carry

    lax.fori_loop(0, NZ, norm_back, 0)
    pg_x = remote(PGX, PGP, ex_s.at[2], ex_r.at[2], partner)
    go(pg_x)
    pg_x.wait_recv()

    def group(ds):
        def pick(ref):
            parts = [ref[d] for d in ds]
            return parts[0] if len(parts) == 1 else jnp.concatenate(parts, axis=0)

        def one(n, carry):
            cols = pl.ds(pl.multiple_of(n * COLS, COLS), COLS)
            out = dot_nt(pick(PGO), WQ[0, cols, :]) + dot_nt(pick(PGP), WQ[1, cols, :])
            for i in range(len(ds)):
                GT[i, :, cols] = out[i * TILE:(i + 1) * TILE]
            return carry

        lax.fori_loop(0, D // COLS, one, 0)

    plan = [(4, 0, None), (3, 1, None), (3, 0, 0), (2, 1, 1), (2, 0, 2), (1, 1, 3), (1, 0, 4)]

    def rs_unit(way, k):
        return remote(SB.at[way, k], RB.at[way, k], rs_s.at[way, k], rs_r.at[way, k], ring_to(way))

    def rs_send(k, slot):
        _, half, needs = plan[k]
        for way in (0, 1):
            h = half if way == 0 else 1 - half
            i = slot[way]
            val = GT[i, h * 32:(h + 1) * 32, :]
            if needs is not None:
                rs_unit(way, needs).wait_recv()
                val = val + RB[way, needs].astype(F32)
            SB[way, k] = val.astype(BF16)
            go(rs_unit(way, k))

    group([4])
    rs_send(0, (0, 0))
    group([3, 5])
    rs_send(1, (0, 1))
    rs_send(2, (0, 1))
    group([2, 6])
    rs_send(3, (0, 1))
    rs_send(4, (0, 1))

    for d in range(1, NZ):
        at_unit(d).wait_recv()

    def out_proj(n, carry):
        cols = pl.ds(pl.multiple_of(n * COLS, COLS), COLS)
        w = WO[:, :, :, :, cols].reshape(NZ * HD, COLS)
        out = dot(AH[...], w)
        AOUT[0, :, cols] = out[:TILE]
        AOUT[1, :, cols] = out[TILE:]
        return carry

    lax.fori_loop(0, D // COLS, out_proj, 0)
    ao_x = remote(AOUT.at[1], AOX, ex_s.at[3], ex_r.at[3], partner)
    go(ao_x)
    group([1, 7])
    rs_send(5, (0, 1))
    rs_send(6, (0, 1))
    ao_x.wait_recv()
    wide_ao = AOUT[0] + AOX[...]
    FO[...] = (Sg[0].reshape(TILE, D).astype(F32) + gate[...] * wide_ao).astype(BF16)
    fo_y = remote(FO, fwd_out, y_s.at[0], y_r.at[0], yn)
    go(fo_y)
    gsum = jnp.sum((UP[0].astype(F32) * wide_ao).reshape(8, 8, D), axis=0)
    for n in range(16):
        GS[n] = gsum[:, n * 192:(n + 1) * 192]

    def g_unit(d, e):
        i = 2 * d + e
        own = dev(d, e)["seq"]
        return remote(GS.at[own], GR.at[2 * ((NZ - d) % NZ) + e], g_s.at[i], g_r.at[i], dev(d, e))

    pairs = [(d, e) for d in range(NZ) for e in range(2) if d or e]
    for d, e in pairs:
        go(g_unit(d, e))
    GR[0] = GS[seq]
    group([0])
    for d, e in pairs:
        g_unit(d, e).wait_recv()
    gate_out[...] = jnp.sum(jnp.sum(GR[...], axis=0), axis=0, keepdims=True)

    def bo_unit(h):
        return remote(BO.at[h], bwd_out.at[h], y_s.at[1 + h], y_r.at[1 + h], yp)

    for h in (1, 0):
        first, second = (5, 6) if h == 1 else (6, 5)
        rs_unit(0, first).wait_recv()
        rs_unit(1, second).wait_recv()
        total = GT[0, h * 32:(h + 1) * 32, :] + RB[0, first].astype(F32) + RB[1, second].astype(F32)
        BO[h] = (UP[0, h * 32:(h + 1) * 32, :].astype(F32) + total).astype(BF16)
        go(bo_unit(h))

    fo_y.wait_recv()
    bo_unit(1).wait_recv()
    bo_unit(0).wait_recv()
    for copy in sent:
        copy.wait_send()


def body(segment_input, output_grad, qkv_weight, out_weight, query_gain, key_gain, gate_scale,
         neighbours, tile_slot):
    dma = pltpu.SemaphoreType.DMA
    vm = pltpu.VMEM
    scratch = [
        vm((NZ, 2, 32, D), BF16),
        vm((2, TILE, D), BF16),
        vm((2 * TILE, D), BF16),
        vm((2, D, 3 * HD), BF16),
        vm((NZ, 4, 2, 16, D), BF16),
        vm((2, NZ, TILE, 3 * HD), F32),
        vm((NZ, TILE, 3 * HD), F32),
        vm((NZ, 16, HD), F32),
        vm((NZ, HD, HD), BF16),
        vm((NZ, HD, HD), BF16),
        vm((NZ, HD, HD), BF16),
        vm((HD, NZ * HD), BF16),
        vm((HD, NZ * HD), BF16),
        vm((NZ, NZ * HD, HD), BF16),
        vm((NZ, HD, HD), BF16),
        vm((HD, NZ * HD), BF16),
        vm((NZ, HD, HD), BF16),
        vm((NZ, HD, HD), BF16),
        vm((NZ, HD, HD), F32),
        vm((NZ * HD, HD), F32),
        vm((NZ * HD, HD), F32),
        vm((NZ, TILE, 3 * HD), BF16),
        vm((NZ, TILE, 3 * HD), BF16),
        vm((NZ, TILE, 3 * HD), BF16),
        vm((2, TILE, D), F32),
        vm((2, 7, 32, D), BF16),
        vm((2, 7, 32, D), BF16),
        vm((2, TILE, D), F32),
        vm((TILE, D), F32),
        vm((TILE, D), BF16),
        vm((2, 32, D), BF16),
        vm((16, 8, 192), F32),
        vm((16, 8, 192), F32),
        dma((4,)), dma((2, 7)), dma((2, 7)), dma((2, 4)), dma((2, 4)), dma((NZ, 4)), dma((NZ, 4)),
        dma((NZ,)), dma((NZ,)), dma((4,)), dma((4,)), dma((NZ,)), dma((NZ,)), dma((NZ,)), dma((NZ,)),
        dma((2, 7)), dma((2, 7)), dma((3,)), dma((3,)), dma((16,)), dma((16,)),
    ]
    any_spec = pl.BlockSpec(memory_space=pl.ANY)
    vm_spec = pl.BlockSpec(memory_space=pltpu.VMEM)
    fwd, bwd, gate = pl.pallas_call(
        kernel,
        name="section",
        out_shape=(
            jax.ShapeDtypeStruct((TILE, D), BF16),
            jax.ShapeDtypeStruct((2, 32, D), BF16),
            jax.ShapeDtypeStruct((1, 192), F32),
        ),
        in_specs=[any_spec] * 4 + [vm_spec] * 5,
        out_specs=(any_spec, any_spec, vm_spec),
        scratch_shapes=scratch,
        compiler_params=pltpu.CompilerParams(
            collective_id=0, has_side_effects=True, vmem_limit_bytes=56 * 1024 * 1024),
    )(
        segment_input.reshape(2, 32, D),
        output_grad.reshape(TILE, D),
        qkv_weight.reshape(D, 3 * HD),
        out_weight.reshape(4, 2, 16, D),
        query_gain, key_gain, gate_scale, neighbours, tile_slot[None],
    )
    return fwd[None], bwd.reshape(1, TILE, D), gate


def solution(mesh):
    in_specs = (
        P("pipe", ("dp", "seq"), None),
        P("pipe", ("dp", "seq"), None),
        P("pipe", None, "seq", None),
        P("pipe", "seq", None),
        P("pipe", None),
        P("pipe", None),
        P("pipe", None),
        P("dp", None),
        P("dp"),
    )
    out_specs = (
        P("pipe", ("dp", "seq"), None),
        P("pipe", ("dp", "seq"), None),
        P(("dp", "pipe"), "seq"),
    )
    return jax.shard_map(body, mesh=mesh, in_specs=in_specs, out_specs=out_specs, check_vma=False)
```

```python
import functools
import math

import jax
import jax.numpy as jnp
from jax import lax
from jax.experimental import pallas as pl
from jax.experimental.pallas import tpu as pltpu
from jax.sharding import PartitionSpec as P

EPSILON = 1e-06
MESH = pl.DeviceIdType.MESH
F32 = jnp.float32
BF16 = jnp.bfloat16
D = 3072
HD = 128
TILE = 64
NZ = 8
QB = 256
NQ = 4
COLS = 512
NT = (((1,), (1,)), ((), ()))


def dot(a, b):
    return jnp.dot(a, b, preferred_element_type=F32)


def dot_nt(a, b):
    return lax.dot_general(a, b, NT, preferred_element_type=F32)


def kernel(
    stream, upstream, wqkv, wout, qgain, kgain, gate, neigh, tslot,
    fwd_out, bwd_out, gate_out,
    Sg, UP, SC, WQ, WO, PJX, PJ1, BIAS, Qb, Kb, Vb, KT, VT, Pb, ATT, AH, DOS, DO,
    dQ, dK, dV, PG, PGX, WT, GT, SB, RB, AOUT, AOX, FO, BO, GS, GR,
    ld, zs_s, zs_r, zw_s, zw_r, xw_s, xw_r, pj_s, pj_r, ex_s, ex_r,
    at_s, at_r, do_s, do_r, pg_s, pg_r, rs_s, rs_r, y_s, y_r, g_s, g_r,
):
    seq = lax.axis_index("seq")
    x = lax.axis_index("dp")
    y = lax.axis_index("pipe")
    z = lax.div(seq, 2)
    c = lax.rem(seq, 2)

    def dev(d, e=0):
        return {"seq": 2 * lax.rem(z + d, NZ) + (c if e == 0 else 1 - c)}

    right, left, partner = dev(1), dev(NZ - 1), dev(0, 1)
    xr = {"dp": lax.rem(x + 1, 4)}
    xl = {"dp": lax.rem(x + 3, 4)}
    yn = {"pipe": lax.rem(y + 1, 4)}
    yp = {"pipe": lax.rem(y + 3, 4)}

    sent = []

    def remote(src, dst, ssem, rsem, to):
        return pltpu.make_async_remote_copy(
            src_ref=src, dst_ref=dst, send_sem=ssem, recv_sem=rsem,
            device_id=to, device_id_type=MESH)

    def go(copy):
        copy.start()
        sent.append(copy)

    loads = [
        pltpu.make_async_copy(wout, WO.at[0], ld.at[0]),
        pltpu.make_async_copy(stream, Sg.at[0], ld.at[1]),
        pltpu.make_async_copy(upstream, UP.at[0], ld.at[2]),
        pltpu.make_async_copy(wqkv, WQ.at[0], ld.at[3]),
    ]
    for copy in loads:
        copy.start()

    barrier = pltpu.get_barrier_semaphore()
    peers = [right, left, partner, xr, xl, yn, yp]
    for peer in peers:
        pl.semaphore_signal(barrier, inc=1, device_id=peer, device_id_type=MESH)
    pl.semaphore_wait(barrier, len(peers))

    def at(way, j):
        return (NZ - j) % NZ if way == 0 else j % NZ

    def ring_to(way):
        return right if way == 0 else left

    def s_unit(way, k):
        j, half = k // 2, (k + way) % 2
        return remote(Sg.at[at(way, j), half], Sg.at[at(way, j + 1), half],
                      zs_s.at[way, k], zs_r.at[way, k], ring_to(way))

    def w_unit(way, k):
        j, half = k // 2, (k + way) % 2
        return remote(WO.at[at(way, j), x, half], WO.at[at(way, j + 1), x, half],
                      zw_s.at[way, k], zw_r.at[way, k], ring_to(way))

    def x_unit(d, way, part):
        quarter = x if part < 2 else lax.rem(x + (3 if way == 0 else 1), 4)
        ref = WO.at[d, quarter, part if part < 2 else way]
        return remote(ref, ref, xw_s.at[d, way, part], xw_r.at[d, way, part], xr if way == 0 else xl)

    def s_wait(k):
        for way in (0, 1):
            s_unit(way, k).wait_recv()

    def s_next(k):
        s_wait(k)
        if k + 2 <= 6:
            for way in (0, 1):
                go(s_unit(way, k + 2))

    def w_next(k):
        for way in (0, 1):
            w_unit(way, k).wait_recv()
            if k + 2 <= 6:
                go(w_unit(way, k + 2))

    def x_send(d, half):
        for way in (0, 1):
            go(x_unit(d, way, half))

    def x_next(d, way):
        x_unit(d, way, way).wait_recv()
        go(x_unit(d, way, 2))

    def x_done(d):
        for way in (0, 1):
            x_unit(d, way, 1 - way).wait_recv()
            x_unit(d, way, 2).wait_recv()

    def project(ds):
        rows = [Sg.at[d] for d in ds]

        def one(e, carry):
            lhs = [r[...].reshape(TILE, D) for r in rows]
            lhs = lhs[0] if len(lhs) == 1 else jnp.concatenate(lhs, axis=0)
            out = dot(lhs, WQ[e])
            for n, d in enumerate(ds):
                PJX[e, d] = out[n * TILE:(n + 1) * TILE]
            return carry

        lax.fori_loop(0, 2, one, 0)
        for d in ds:
            go(pj_unit(d))

    def pj_unit(d):
        return remote(PJX.at[1, d], PJ1.at[d], pj_s.at[d], pj_r.at[d], partner)

    def do_unit(d):
        return remote(DOS.at[d], DO.at[(NZ - d) % NZ], do_s.at[d], do_r.at[d], dev(d))

    def grads_in(ds):
        for d in ds:
            val = dot_nt(SC[...], WO[d].reshape(HD, D)).astype(BF16)
            if d == 0:
                DO[0] = val
            else:
                DOS[d] = val
                go(do_unit(d))

    up_x = remote(UP.at[0], UP.at[1], ex_s.at[0], ex_r.at[0], partner)
    wq_x = remote(WQ.at[0], WQ.at[1], ex_s.at[1], ex_r.at[1], partner)

    loads[0].wait()
    for k in (0, 1):
        for way in (0, 1):
            go(w_unit(way, k))
    loads[1].wait()
    for k in (0, 1):
        for way in (0, 1):
            go(s_unit(way, k))
    loads[2].wait()
    go(up_x)
    loads[3].wait()
    go(wq_x)

    i_rows = lax.broadcasted_iota(jnp.int32, (16, 16), 0)
    rel_z = z + lax.div(i_rows, 2)
    rel_z = jnp.where(rel_z >= NZ, rel_z - NZ, rel_z)
    odd = lax.rem(i_rows, 2)
    rel_slot = 2 * rel_z + jnp.where(odd == 0, c, 1 - c)
    lanes16 = lax.broadcasted_iota(jnp.int32, (16, 16), 1)
    listed = jnp.zeros((16, 16), F32)
    for k in range(neigh.shape[1]):
        listed = listed + jnp.where(neigh[:, k:k + 1] == lanes16, 1.0, 0.0)
    holds = jnp.where(rel_slot == tslot[...], 1.0, 0.0)
    by_key = dot_nt(holds, listed)
    by_key = dot_nt(by_key, holds)
    spread = jnp.where(
        lax.div(lax.broadcasted_iota(jnp.int32, (16, 1024), 1), TILE)
        == lax.broadcasted_iota(jnp.int32, (16, 1024), 0), 1.0, 0.0)
    bias = jnp.where(dot(by_key, spread) > 0.5, 0.0, -jnp.inf)
    for n in range(NQ):
        BIAS[n] = bias[:, n * QB:(n + 1) * QB]

    def both(d):
        return jnp.concatenate([PJX[0, d], PJ1[d]], axis=0)

    def unit_of(part):
        spread = jnp.sqrt(jnp.mean(part * part, axis=-1, keepdims=True) + EPSILON)
        return part / spread, spread

    def norm(ds):
        for d in ds:
            pj_unit(d).wait_recv()
            pj = both(d)
            q_unit, _ = unit_of(pj[:, :HD])
            k_unit, _ = unit_of(pj[:, HD:2 * HD])
            Qb[d] = (q_unit * qgain[...]).astype(BF16)
            k = k_unit * kgain[...]
            v = pj[:, 2 * HD:]
            Kb[d] = k.astype(BF16)
            Vb[d] = v.astype(BF16)
            KT[:, d * HD:(d + 1) * HD] = k.T.astype(BF16)
            VT[:, d * HD:(d + 1) * HD] = v.T.astype(BF16)

    w_next(0)
    x_send(7, 0)
    x_send(1, 1)
    up_x.wait_recv()
    SC[...] = (UP[...].astype(F32) * gate[...]).astype(BF16).reshape(2 * TILE, D)
    w_next(1)
    x_send(7, 1)
    x_send(1, 0)
    wq_x.wait_recv()
    project([0])
    x_next(7, 0)
    x_next(1, 1)
    s_next(0)
    grads_in([0])
    x_next(1, 0)
    x_next(7, 1)

    def flip(e):
        def one(n, carry):
            rows = pl.ds(pl.multiple_of(n * COLS, COLS), COLS)
            WT[e * 3 * HD:(e + 1) * 3 * HD, rows] = WQ[e, rows, :].T
            return carry

        lax.fori_loop(0, D // COLS, one, 0)

    s_next(1)
    project([7, 1])
    w_next(2)
    x_send(6, 0)
    x_send(2, 1)
    x_done(7)
    x_done(1)
    w_next(3)
    x_send(6, 1)
    x_send(2, 0)
    grads_in([7, 1])
    x_next(6, 0)
    x_next(2, 1)
    flip(0)
    s_next(2)
    norm([0, 7, 1])
    x_next(2, 0)
    x_next(6, 1)
    s_next(3)
    project([6, 2])
    w_next(4)
    x_send(5, 0)
    x_send(3, 1)
    x_done(6)
    x_done(2)
    w_next(5)
    x_send(5, 1)
    x_send(3, 0)
    grads_in([6, 2])
    x_next(5, 0)
    x_next(3, 1)
    flip(1)
    s_next(4)
    norm([6, 2])
    x_next(3, 0)
    x_next(5, 1)
    s_next(5)
    project([5, 3])
    w_next(6)
    x_send(4, 0)
    x_send(4, 1)
    x_done(5)
    x_done(3)
    grads_in([5, 3])
    x_next(4, 0)
    x_next(4, 1)
    norm([5, 3])
    s_next(6)
    project([4])
    norm([4])
    scale = 1.0 / math.sqrt(HD)

    def block(ref, n):
        return ref[pl.ds(2 * n, 2)].reshape(QB, HD)

    def attend(n, carry):
        s = dot_nt(Kb[...].reshape(NZ * HD, HD), block(Qb, n)) * (scale * math.log2(math.e))
        s = s.reshape(16, TILE, QB) + BIAS[n][:, None, :]
        s = s.reshape(NZ * HD, QB)
        p = jnp.exp2(s - jnp.max(s, axis=0, keepdims=True))
        p = (p * (1.0 / jnp.sum(p, axis=0, keepdims=True))).astype(BF16)
        Pb[n] = p
        ATT[pl.ds(2 * n, 2)] = dot(VT[...], p).T.astype(BF16).reshape(2, HD, HD)
        return carry

    lax.fori_loop(0, 2, attend, 0)
    x_done(4)
    grads_in([4])
    lax.fori_loop(2, NQ, attend, 0)

    def at_unit(d):
        back = (NZ - d) % NZ
        return remote(ATT.at[d], AH.at[:, back * HD:(back + 1) * HD], at_s.at[d], at_r.at[d], dev(d))

    for d in range(1, NZ):
        go(at_unit(d))
    AH[:, :HD] = ATT[0]
    dK[...] = jnp.zeros_like(dK)
    dV[...] = jnp.zeros_like(dV)
    for d in range(1, NZ):
        do_unit(d).wait_recv()

    def attend_back(n, carry):
        grad, p = block(DO, n), Pb[n]
        dV[...] += dot(p, grad)
        dp = dot_nt(Vb[...].reshape(NZ * HD, HD), grad)
        wide = p.astype(F32)
        delta = jnp.sum(wide * dp, axis=0, keepdims=True)
        ds = (wide * (dp - delta) * scale).astype(BF16)
        dK[...] += dot(ds, block(Qb, n))
        dQ[pl.ds(2 * n, 2)] = dot(KT[...], ds).T.reshape(2, HD, HD)
        return carry

    lax.fori_loop(0, NQ, attend_back, 0)

    def norm_back(ds):
        for d in ds:
            pj = both(d)

            def one(part, grad, gain):
                unit, spread = unit_of(part)
                a = grad * gain
                return (a - unit * jnp.mean(a * unit, axis=-1, keepdims=True)) / spread

            gq = one(pj[:, :HD], dQ[d], qgain[...])
            gk = one(pj[:, HD:2 * HD], dK[d * HD:(d + 1) * HD, :], kgain[...])
            pg = jnp.concatenate([gq, gk, dV[d * HD:(d + 1) * HD, :]], axis=1).astype(BF16)
            PG[d, :, :3 * HD] = pg[:TILE]
            PGX[d] = pg[TILE:]
            go(pg_unit(d))

    def pg_unit(d):
        return remote(PGX.at[d], PG.at[d, :, 3 * HD:], pg_s.at[d], pg_r.at[d], partner)

    norm_back([4, 3, 5])

    def group(ds):
        for d in ds:
            pg_unit(d).wait_recv()

        def one(n, carry):
            cols = pl.ds(pl.multiple_of(n * COLS, COLS), COLS)
            rows = jnp.concatenate([PG[d] for d in ds], axis=0)
            out = dot(rows, WT[:, cols])
            for i, d in enumerate(ds):
                GT[d, :, cols] = out[i * TILE:(i + 1) * TILE]
            return carry

        lax.fori_loop(0, D // COLS, one, 0)

    ends = [(1, 2), (1, 3), (1, 0), (1, 1)]
    plan = [
        [(4, 0), (4, 1), (3, 2), (3, 3), (3, 0), (3, 1), (2, 2), (2, 3), (2, 0), (2, 1)] + ends,
        [(4, 2), (4, 3), (3, 0), (3, 1), (3, 2), (3, 3), (2, 0), (2, 1), (2, 2), (2, 3)] + ends,
    ]

    def rs_unit(way, k):
        return remote(SB.at[way, k], RB.at[way, k], rs_s.at[way, k], rs_r.at[way, k], ring_to(way))

    def rs_send(k):
        for way in (0, 1):
            dist, q = plan[way][k]
            val = GT[dist if way == 0 else NZ - dist, q * 16:(q + 1) * 16, :]
            if (dist + 1, q) in plan[way]:
                needs = plan[way].index((dist + 1, q))
                rs_unit(way, needs).wait_recv()
                val = val + RB[way, needs].astype(F32)
            SB[way, k] = val.astype(BF16)
            go(rs_unit(way, k))

    group([4, 3, 5])
    rs_send(0)
    rs_send(1)
    rs_send(2)
    rs_send(3)
    norm_back([2, 6, 1, 7, 0])
    rs_send(4)
    rs_send(5)
    group([2, 6, 1, 7, 0])
    rs_send(6)
    rs_send(7)

    for d in range(1, NZ):
        at_unit(d).wait_recv()

    def out_proj(n, carry):
        cols = pl.ds(pl.multiple_of(n * COLS, COLS), COLS)
        w = WO[:, :, :, :, cols].reshape(NZ * HD, COLS)
        out = dot(AH[...], w)
        AOUT[0, :, cols] = out[:TILE]
        AOUT[1, :, cols] = out[TILE:]
        return carry

    lax.fori_loop(0, 3, out_proj, 0)
    rs_send(8)
    lax.fori_loop(3, D // COLS, out_proj, 0)
    rs_send(9)
    ao_x = remote(AOUT.at[1], AOX, ex_s.at[3], ex_r.at[3], partner)
    go(ao_x)
    ao_x.wait_recv()
    wide_ao = AOUT[0] + AOX[...]
    FO[...] = (Sg[0].reshape(TILE, D).astype(F32) + gate[...] * wide_ao).astype(BF16)
    fo_y = remote(FO, fwd_out, y_s.at[0], y_r.at[0], yn)
    go(fo_y)
    gsum = jnp.sum((UP[0].astype(F32) * wide_ao).reshape(8, 8, D), axis=0)
    for n in range(16):
        GS[n] = gsum[:, n * 192:(n + 1) * 192]

    def g_unit(d, e):
        i = 2 * d + e
        own = dev(d, e)["seq"]
        return remote(GS.at[own], GR.at[2 * ((NZ - d) % NZ) + e], g_s.at[i], g_r.at[i], dev(d, e))

    pairs = [(d, e) for d in range(NZ) for e in range(2) if d or e]
    for d, e in pairs:
        go(g_unit(d, e))
    GR[0] = GS[seq]
    rs_send(10)
    rs_send(11)
    rs_send(12)
    rs_send(13)

    def bo_unit(q):
        return remote(BO.at[q], bwd_out.at[q], y_s.at[1 + q], y_r.at[1 + q], yp)

    for dist, q in ends:
        total = GT[0, q * 16:(q + 1) * 16, :]
        for way in (0, 1):
            k = plan[way].index((dist, q))
            rs_unit(way, k).wait_recv()
            total = total + RB[way, k].astype(F32)
        BO[q] = (UP[0, q * 16:(q + 1) * 16, :].astype(F32) + total).astype(BF16)
        go(bo_unit(q))

    for d, e in pairs:
        g_unit(d, e).wait_recv()
    gate_out[...] = jnp.sum(jnp.sum(GR[...], axis=0), axis=0, keepdims=True)
    fo_y.wait_recv()
    for q in range(4):
        bo_unit(q).wait_recv()
    for copy in sent:
        copy.wait_send()


def body(segment_input, output_grad, qkv_weight, out_weight, query_gain, key_gain, gate_scale,
         neighbours, tile_slot):
    dma = pltpu.SemaphoreType.DMA
    vm = pltpu.VMEM
    scratch = [
        vm((NZ, 2, 32, D), BF16),
        vm((2, TILE, D), BF16),
        vm((2 * TILE, D), BF16),
        vm((2, D, 3 * HD), BF16),
        vm((NZ, 4, 2, 16, D), BF16),
        vm((2, NZ, TILE, 3 * HD), F32),
        vm((NZ, TILE, 3 * HD), F32),
        vm((NQ, 16, QB), F32),
        vm((NZ, HD, HD), BF16),
        vm((NZ, HD, HD), BF16),
        vm((NZ, HD, HD), BF16),
        vm((HD, NZ * HD), BF16),
        vm((HD, NZ * HD), BF16),
        vm((NQ, NZ * HD, QB), BF16),
        vm((NZ, HD, HD), BF16),
        vm((HD, NZ * HD), BF16),
        vm((NZ, HD, HD), BF16),
        vm((NZ, HD, HD), BF16),
        vm((NZ, HD, HD), F32),
        vm((NZ * HD, HD), F32),
        vm((NZ * HD, HD), F32),
        vm((NZ, TILE, 6 * HD), BF16),
        vm((NZ, TILE, 3 * HD), BF16),
        vm((6 * HD, D), BF16),
        vm((NZ, TILE, D), F32),
        vm((2, 14, 16, D), BF16),
        vm((2, 14, 16, D), BF16),
        vm((2, TILE, D), F32),
        vm((TILE, D), F32),
        vm((TILE, D), BF16),
        vm((4, 16, D), BF16),
        vm((16, 8, 192), F32),
        vm((16, 8, 192), F32),
        dma((4,)), dma((2, 7)), dma((2, 7)), dma((2, 7)), dma((2, 7)), dma((NZ, 2, 3)), dma((NZ, 2, 3)),
        dma((NZ,)), dma((NZ,)), dma((4,)), dma((4,)), dma((NZ,)), dma((NZ,)), dma((NZ,)), dma((NZ,)),
        dma((NZ,)), dma((NZ,)), dma((2, 14)), dma((2, 14)), dma((5,)), dma((5,)), dma((16,)), dma((16,)),
    ]
    any_spec = pl.BlockSpec(memory_space=pl.ANY)
    vm_spec = pl.BlockSpec(memory_space=pltpu.VMEM)
    fwd, bwd, gate = pl.pallas_call(
        kernel,
        name="section",
        out_shape=(
            jax.ShapeDtypeStruct((TILE, D), BF16),
            jax.ShapeDtypeStruct((4, 16, D), BF16),
            jax.ShapeDtypeStruct((1, 192), F32),
        ),
        in_specs=[any_spec] * 4 + [vm_spec] * 5,
        out_specs=(any_spec, any_spec, vm_spec),
        scratch_shapes=scratch,
        compiler_params=pltpu.CompilerParams(
            collective_id=0, has_side_effects=True, vmem_limit_bytes=56 * 1024 * 1024),
    )(
        segment_input.reshape(2, 32, D),
        output_grad.reshape(TILE, D),
        qkv_weight.reshape(D, 3 * HD),
        out_weight.reshape(4, 2, 16, D),
        query_gain, key_gain, gate_scale, neighbours, tile_slot[None],
    )
    return fwd[None], bwd.reshape(1, TILE, D), gate


def solution(mesh):
    in_specs = (
        P("pipe", ("dp", "seq"), None),
        P("pipe", ("dp", "seq"), None),
        P("pipe", None, "seq", None),
        P("pipe", "seq", None),
        P("pipe", None),
        P("pipe", None),
        P("pipe", None),
        P("dp", None),
        P("dp"),
    )
    out_specs = (
        P("pipe", ("dp", "seq"), None),
        P("pipe", ("dp", "seq"), None),
        P(("dp", "pipe"), "seq"),
    )
    return jax.shard_map(body, mesh=mesh, in_specs=in_specs, out_specs=out_specs, check_vma=False)
```

```python
import functools
import math

import jax
import jax.numpy as jnp
from jax import lax
from jax.experimental import pallas as pl
from jax.experimental.pallas import tpu as pltpu
from jax.sharding import PartitionSpec as P

EPSILON = 1e-06
MESH = pl.DeviceIdType.MESH
F32 = jnp.float32
BF16 = jnp.bfloat16
D = 3072
HD = 128
TILE = 64
NZ = 8
QB = 256
NQ = 4
COLS = 512
NT = (((1,), (1,)), ((), ()))


def dot(a, b):
    return jnp.dot(a, b, preferred_element_type=F32)


def dot_nt(a, b):
    return lax.dot_general(a, b, NT, preferred_element_type=F32)


def kernel(
    stream, upstream, wqkv, wout, qgain, kgain, gate, neigh, tslot,
    fwd_out, bwd_out, gate_out,
    Sg, UP, SC, WQ, WO, PJX, PJ1, BIAS, Qb, Kb, Vb, KT, VT, Pb, ATT, AH, DOS, DO,
    dQ, dK, dV, PG, PGX, WT, GT, SB, RB, AOUT, AOX, FO, BO, GS, GR,
    ld, zs_s, zs_r, zw_s, zw_r, xw_s, xw_r, pj_s, pj_r, ex_s, ex_r,
    at_s, at_r, do_s, do_r, pg_s, pg_r, rs_s, rs_r, y_s, y_r, g_s, g_r,
):
    seq = lax.axis_index("seq")
    x = lax.axis_index("dp")
    y = lax.axis_index("pipe")
    z = lax.div(seq, 2)
    c = lax.rem(seq, 2)

    def dev(d, e=0):
        return {"seq": 2 * lax.rem(z + d, NZ) + (c if e == 0 else 1 - c)}

    right, left, partner = dev(1), dev(NZ - 1), dev(0, 1)
    xr = {"dp": lax.rem(x + 1, 4)}
    xl = {"dp": lax.rem(x + 3, 4)}
    yn = {"pipe": lax.rem(y + 1, 4)}
    yp = {"pipe": lax.rem(y + 3, 4)}

    sent = []

    def remote(src, dst, ssem, rsem, to):
        return pltpu.make_async_remote_copy(
            src_ref=src, dst_ref=dst, send_sem=ssem, recv_sem=rsem,
            device_id=to, device_id_type=MESH)

    def go(copy):
        copy.start()
        sent.append(copy)

    loads = [
        pltpu.make_async_copy(wout, WO.at[0], ld.at[0]),
        pltpu.make_async_copy(stream, Sg.at[0], ld.at[1]),
        pltpu.make_async_copy(upstream, UP.at[0], ld.at[2]),
        pltpu.make_async_copy(wqkv, WQ.at[0], ld.at[3]),
    ]
    for copy in loads:
        copy.start()

    barrier = pltpu.get_barrier_semaphore()
    peers = [right, left, partner, xr, xl, yn, yp]
    for peer in peers:
        pl.semaphore_signal(barrier, inc=1, device_id=peer, device_id_type=MESH)
    pl.semaphore_wait(barrier, len(peers))

    def at(way, j):
        return (NZ - j) % NZ if way == 0 else j % NZ

    def ring_to(way):
        return right if way == 0 else left

    def s_unit(way, k):
        j, half = k // 2, (k + way) % 2
        return remote(Sg.at[at(way, j), half], Sg.at[at(way, j + 1), half],
                      zs_s.at[way, k], zs_r.at[way, k], ring_to(way))

    def w_unit(way, k):
        j, half = k // 2, (k + way) % 2
        return remote(WO.at[at(way, j), x, half], WO.at[at(way, j + 1), x, half],
                      zw_s.at[way, k], zw_r.at[way, k], ring_to(way))

    def x_unit(d, way, part):
        quarter = x if part < 2 else lax.rem(x + (3 if way == 0 else 1), 4)
        ref = WO.at[d, quarter, part if part < 2 else way]
        return remote(ref, ref, xw_s.at[d, way, part], xw_r.at[d, way, part], xr if way == 0 else xl)

    def s_wait(k):
        for way in (0, 1):
            s_unit(way, k).wait_recv()

    def s_next(k):
        s_wait(k)
        if k + 2 <= 6:
            for way in (0, 1):
                go(s_unit(way, k + 2))

    def w_next(k):
        for way in (0, 1):
            w_unit(way, k).wait_recv()
            if k + 2 <= 6:
                go(w_unit(way, k + 2))

    def x_send(d, half):
        for way in (0, 1):
            go(x_unit(d, way, half))

    def x_both(d):
        for half in (0, 1):
            for way in (0, 1):
                go(x_unit(d, way, (half + way) % 2))

    def x_next(d, way):
        x_unit(d, way, way).wait_recv()
        go(x_unit(d, way, 2))

    def x_done(d):
        for way in (0, 1):
            x_unit(d, way, 1 - way).wait_recv()
            x_unit(d, way, 2).wait_recv()

    def project(ds):
        rows = [Sg.at[d] for d in ds]

        def one(e, carry):
            lhs = [r[...].reshape(TILE, D) for r in rows]
            lhs = lhs[0] if len(lhs) == 1 else jnp.concatenate(lhs, axis=0)
            out = dot(lhs, WQ[e])
            for n, d in enumerate(ds):
                PJX[e, d] = out[n * TILE:(n + 1) * TILE]
            return carry

        lax.fori_loop(0, 2, one, 0)
        for d in ds:
            go(pj_unit(d))

    def pj_unit(d):
        return remote(PJX.at[1, d], PJ1.at[d], pj_s.at[d], pj_r.at[d], partner)

    def do_unit(d):
        return remote(DOS.at[d], DO.at[(NZ - d) % NZ], do_s.at[d], do_r.at[d], dev(d))

    def grads_in(ds):
        for d in ds:
            val = dot_nt(SC[...], WO[d].reshape(HD, D)).astype(BF16)
            if d == 0:
                DO[0] = val
            else:
                DOS[d] = val
                go(do_unit(d))

    up_x = remote(UP.at[0], UP.at[1], ex_s.at[0], ex_r.at[0], partner)
    wq_x = remote(WQ.at[0], WQ.at[1], ex_s.at[1], ex_r.at[1], partner)

    loads[0].wait()
    for k in (0, 1):
        for way in (0, 1):
            go(w_unit(way, k))
    loads[1].wait()
    loads[2].wait()
    go(up_x)
    loads[3].wait()
    go(wq_x)

    i_rows = lax.broadcasted_iota(jnp.int32, (16, 16), 0)
    rel_z = z + lax.div(i_rows, 2)
    rel_z = jnp.where(rel_z >= NZ, rel_z - NZ, rel_z)
    odd = lax.rem(i_rows, 2)
    rel_slot = 2 * rel_z + jnp.where(odd == 0, c, 1 - c)
    lanes16 = lax.broadcasted_iota(jnp.int32, (16, 16), 1)
    listed = jnp.zeros((16, 16), F32)
    for k in range(neigh.shape[1]):
        listed = listed + jnp.where(neigh[:, k:k + 1] == lanes16, 1.0, 0.0)
    holds = jnp.where(rel_slot == tslot[...], 1.0, 0.0)
    by_key = dot_nt(holds, listed)
    by_key = dot_nt(by_key, holds)
    spread = jnp.where(
        lax.div(lax.broadcasted_iota(jnp.int32, (16, 1024), 1), TILE)
        == lax.broadcasted_iota(jnp.int32, (16, 1024), 0), 1.0, 0.0)
    bias = jnp.where(dot(by_key, spread) > 0.5, 0.0, -jnp.inf)
    for n in range(NQ):
        BIAS[n] = bias[:, n * QB:(n + 1) * QB]

    def both(d):
        return jnp.concatenate([PJX[0, d], PJ1[d]], axis=0)

    def unit_of(part):
        spread = jnp.sqrt(jnp.mean(part * part, axis=-1, keepdims=True) + EPSILON)
        return part / spread, spread

    def norm(ds):
        for d in ds:
            pj_unit(d).wait_recv()
            pj = both(d)
            q_unit, _ = unit_of(pj[:, :HD])
            k_unit, _ = unit_of(pj[:, HD:2 * HD])
            Qb[d] = (q_unit * qgain[...]).astype(BF16)
            k = k_unit * kgain[...]
            v = pj[:, 2 * HD:]
            Kb[d] = k.astype(BF16)
            Vb[d] = v.astype(BF16)
            KT[:, d * HD:(d + 1) * HD] = k.T.astype(BF16)
            VT[:, d * HD:(d + 1) * HD] = v.T.astype(BF16)

    def flip(e):
        def one(n, carry):
            rows = pl.ds(pl.multiple_of(n * COLS, COLS), COLS)
            WT[e * 3 * HD:(e + 1) * 3 * HD, rows] = WQ[e, rows, :].T
            return carry

        lax.fori_loop(0, D // COLS, one, 0)

    w_next(0)
    x_send(7, 0)
    w_next(1)
    x_send(7, 1)
    for k in (0, 1):
        for way in (0, 1):
            go(s_unit(way, k))
    up_x.wait_recv()
    SC[...] = (UP[...].astype(F32) * gate[...]).astype(BF16).reshape(2 * TILE, D)
    x_next(7, 0)
    w_next(2)
    x_send(6, 0)
    x_send(2, 1)
    x_next(7, 1)
    w_next(3)
    x_send(6, 1)
    x_send(2, 0)
    wq_x.wait_recv()
    project([0])
    grads_in([0])
    x_next(6, 0)
    x_next(2, 1)
    s_next(0)
    x_done(7)
    grads_in([7])
    x_next(2, 0)
    x_next(6, 1)
    s_next(1)
    project([7, 1])
    w_next(4)
    x_send(5, 0)
    x_send(3, 1)
    w_next(5)
    x_send(5, 1)
    x_send(3, 0)
    flip(0)
    x_done(6)
    x_done(2)
    grads_in([6, 2])
    s_next(2)
    x_next(5, 0)
    x_next(3, 1)
    norm([0, 7, 1])
    x_next(3, 0)
    x_next(5, 1)
    s_next(3)
    project([6, 2])
    w_next(6)
    x_both(4)
    x_both(1)
    flip(1)
    x_done(5)
    x_done(3)
    grads_in([5, 3])
    s_next(4)
    norm([6, 2])
    x_next(4, 0)
    x_next(4, 1)
    s_next(5)
    project([5, 3])
    x_next(1, 0)
    x_next(1, 1)
    x_done(4)
    grads_in([4])
    norm([5, 3])
    s_next(6)
    project([4])
    norm([4])
    scale = 1.0 / math.sqrt(HD)

    def block(ref, n):
        return ref[pl.ds(2 * n, 2)].reshape(QB, HD)

    def attend(n, carry):
        s = dot_nt(Kb[...].reshape(NZ * HD, HD), block(Qb, n)) * (scale * math.log2(math.e))
        s = s.reshape(16, TILE, QB) + BIAS[n][:, None, :]
        s = s.reshape(NZ * HD, QB)
        p = jnp.exp2(s - jnp.max(s, axis=0, keepdims=True))
        p = (p * (1.0 / jnp.sum(p, axis=0, keepdims=True))).astype(BF16)
        Pb[n] = p
        ATT[pl.ds(2 * n, 2)] = dot(VT[...], p).T.astype(BF16).reshape(2, HD, HD)
        return carry

    lax.fori_loop(0, 2, attend, 0)
    x_done(1)
    grads_in([1])
    lax.fori_loop(2, NQ, attend, 0)

    def at_unit(d):
        back = (NZ - d) % NZ
        return remote(ATT.at[d], AH.at[:, back * HD:(back + 1) * HD], at_s.at[d], at_r.at[d], dev(d))

    for d in range(1, NZ):
        go(at_unit(d))
    AH[:, :HD] = ATT[0]
    dK[...] = jnp.zeros_like(dK)
    dV[...] = jnp.zeros_like(dV)
    for d in (7, 6, 5, 4, 3):
        do_unit(d).wait_recv()

    def attend_back(n, carry):
        grad, p = block(DO, n), Pb[n]
        dV[...] += dot(p, grad)
        dp = dot_nt(Vb[...].reshape(NZ * HD, HD), grad)
        wide = p.astype(F32)
        delta = jnp.sum(wide * dp, axis=0, keepdims=True)
        ds = (wide * (dp - delta) * scale).astype(BF16)
        dK[...] += dot(ds, block(Qb, n))
        dQ[pl.ds(2 * n, 2)] = dot(KT[...], ds).T.reshape(2, HD, HD)
        return carry

    lax.fori_loop(0, NQ - 1, attend_back, 0)
    for d in (2, 1):
        do_unit(d).wait_recv()
    attend_back(NQ - 1, 0)

    def norm_back(ds):
        for d in ds:
            pj = both(d)

            def one(part, grad, gain):
                unit, spread = unit_of(part)
                a = grad * gain
                return (a - unit * jnp.mean(a * unit, axis=-1, keepdims=True)) / spread

            gq = one(pj[:, :HD], dQ[d], qgain[...])
            gk = one(pj[:, HD:2 * HD], dK[d * HD:(d + 1) * HD, :], kgain[...])
            pg = jnp.concatenate([gq, gk, dV[d * HD:(d + 1) * HD, :]], axis=1).astype(BF16)
            PG[d, :, :3 * HD] = pg[:TILE]
            PGX[d] = pg[TILE:]
            go(pg_unit(d))

    def pg_unit(d):
        return remote(PGX.at[d], PG.at[d, :, 3 * HD:], pg_s.at[d], pg_r.at[d], partner)

    norm_back([4, 3, 5])

    def group(ds):
        for d in ds:
            pg_unit(d).wait_recv()

        def one(n, carry):
            cols = pl.ds(pl.multiple_of(n * COLS, COLS), COLS)
            rows = jnp.concatenate([PG[d] for d in ds], axis=0)
            out = dot(rows, WT[:, cols])
            for i, d in enumerate(ds):
                GT[d, :, cols] = out[i * TILE:(i + 1) * TILE]
            return carry

        lax.fori_loop(0, D // COLS, one, 0)

    ends = [(1, 2), (1, 3), (1, 0), (1, 1)]
    plan = [
        [(4, 0), (4, 1), (3, 2), (3, 3), (3, 0), (3, 1), (2, 2), (2, 3), (2, 0), (2, 1)] + ends,
        [(4, 2), (4, 3), (3, 0), (3, 1), (3, 2), (3, 3), (2, 0), (2, 1), (2, 2), (2, 3)] + ends,
    ]

    def rs_unit(way, k):
        return remote(SB.at[way, k], RB.at[way, k], rs_s.at[way, k], rs_r.at[way, k], ring_to(way))

    def rs_send(k):
        for way in (0, 1):
            dist, q = plan[way][k]
            val = GT[dist if way == 0 else NZ - dist, q * 16:(q + 1) * 16, :]
            if (dist + 1, q) in plan[way]:
                needs = plan[way].index((dist + 1, q))
                rs_unit(way, needs).wait_recv()
                val = val + RB[way, needs].astype(F32)
            SB[way, k] = val.astype(BF16)
            go(rs_unit(way, k))

    group([4, 3, 5])
    rs_send(0)
    rs_send(1)
    rs_send(2)
    rs_send(3)
    norm_back([2, 6, 1, 7, 0])
    rs_send(4)
    rs_send(5)
    group([2, 6, 1, 7, 0])
    rs_send(6)
    rs_send(7)

    rs_send(8)
    rs_send(9)

    for d in range(1, NZ):
        at_unit(d).wait_recv()

    def out_proj(n, carry):
        cols = pl.ds(pl.multiple_of(n * COLS, COLS), COLS)
        w = WO[:, :, :, :, cols].reshape(NZ * HD, COLS)
        out = dot(AH[...], w)
        AOUT[0, :, cols] = out[:TILE]
        AOUT[1, :, cols] = out[TILE:]
        return carry

    lax.fori_loop(0, D // COLS, out_proj, 0)
    ao_x = remote(AOUT.at[1], AOX, ex_s.at[3], ex_r.at[3], partner)
    go(ao_x)
    rs_send(10)
    rs_send(11)
    rs_send(12)
    rs_send(13)
    ao_x.wait_recv()
    wide_ao = AOUT[0] + AOX[...]
    FO[...] = (Sg[0].reshape(TILE, D).astype(F32) + gate[...] * wide_ao).astype(BF16)
    fo_y = remote(FO, fwd_out, y_s.at[0], y_r.at[0], yn)
    go(fo_y)
    gsum = jnp.sum((UP[0].astype(F32) * wide_ao).reshape(8, 8, D), axis=0)
    for n in range(16):
        GS[n] = gsum[:, n * 192:(n + 1) * 192]

    def g_unit(d, e):
        i = 2 * d + e
        own = dev(d, e)["seq"]
        return remote(GS.at[own], GR.at[2 * ((NZ - d) % NZ) + e], g_s.at[i], g_r.at[i], dev(d, e))

    pairs = [(d, e) for d in range(NZ) for e in range(2) if d or e]
    for d, e in pairs:
        go(g_unit(d, e))
    GR[0] = GS[seq]

    def bo_unit(q):
        return remote(BO.at[q], bwd_out.at[q], y_s.at[1 + q], y_r.at[1 + q], yp)

    for dist, q in ends:
        total = GT[0, q * 16:(q + 1) * 16, :]
        for way in (0, 1):
            k = plan[way].index((dist, q))
            rs_unit(way, k).wait_recv()
            total = total + RB[way, k].astype(F32)
        BO[q] = (UP[0, q * 16:(q + 1) * 16, :].astype(F32) + total).astype(BF16)
        go(bo_unit(q))

    for d, e in pairs:
        g_unit(d, e).wait_recv()
    gate_out[...] = jnp.sum(jnp.sum(GR[...], axis=0), axis=0, keepdims=True)
    fo_y.wait_recv()
    for q in range(4):
        bo_unit(q).wait_recv()
    for copy in sent:
        copy.wait_send()


def body(segment_input, output_grad, qkv_weight, out_weight, query_gain, key_gain, gate_scale,
         neighbours, tile_slot):
    dma = pltpu.SemaphoreType.DMA
    vm = pltpu.VMEM
    scratch = [
        vm((NZ, 2, 32, D), BF16),
        vm((2, TILE, D), BF16),
        vm((2 * TILE, D), BF16),
        vm((2, D, 3 * HD), BF16),
        vm((NZ, 4, 2, 16, D), BF16),
        vm((2, NZ, TILE, 3 * HD), F32),
        vm((NZ, TILE, 3 * HD), F32),
        vm((NQ, 16, QB), F32),
        vm((NZ, HD, HD), BF16),
        vm((NZ, HD, HD), BF16),
        vm((NZ, HD, HD), BF16),
        vm((HD, NZ * HD), BF16),
        vm((HD, NZ * HD), BF16),
        vm((NQ, NZ * HD, QB), BF16),
        vm((NZ, HD, HD), BF16),
        vm((HD, NZ * HD), BF16),
        vm((NZ, HD, HD), BF16),
        vm((NZ, HD, HD), BF16),
        vm((NZ, HD, HD), F32),
        vm((NZ * HD, HD), F32),
        vm((NZ * HD, HD), F32),
        vm((NZ, TILE, 6 * HD), BF16),
        vm((NZ, TILE, 3 * HD), BF16),
        vm((6 * HD, D), BF16),
        vm((NZ, TILE, D), F32),
        vm((2, 14, 16, D), BF16),
        vm((2, 14, 16, D), BF16),
        vm((2, TILE, D), F32),
        vm((TILE, D), F32),
        vm((TILE, D), BF16),
        vm((4, 16, D), BF16),
        vm((16, 8, 192), F32),
        vm((16, 8, 192), F32),
        dma((4,)), dma((2, 7)), dma((2, 7)), dma((2, 7)), dma((2, 7)), dma((NZ, 2, 3)), dma((NZ, 2, 3)),
        dma((NZ,)), dma((NZ,)), dma((4,)), dma((4,)), dma((NZ,)), dma((NZ,)), dma((NZ,)), dma((NZ,)),
        dma((NZ,)), dma((NZ,)), dma((2, 14)), dma((2, 14)), dma((5,)), dma((5,)), dma((16,)), dma((16,)),
    ]
    any_spec = pl.BlockSpec(memory_space=pl.ANY)
    vm_spec = pl.BlockSpec(memory_space=pltpu.VMEM)
    fwd, bwd, gate = pl.pallas_call(
        kernel,
        name="section",
        out_shape=(
            jax.ShapeDtypeStruct((TILE, D), BF16),
            jax.ShapeDtypeStruct((4, 16, D), BF16),
            jax.ShapeDtypeStruct((1, 192), F32),
        ),
        in_specs=[any_spec] * 4 + [vm_spec] * 5,
        out_specs=(any_spec, any_spec, vm_spec),
        scratch_shapes=scratch,
        compiler_params=pltpu.CompilerParams(
            collective_id=0, has_side_effects=True, vmem_limit_bytes=56 * 1024 * 1024),
    )(
        segment_input.reshape(2, 32, D),
        output_grad.reshape(TILE, D),
        qkv_weight.reshape(D, 3 * HD),
        out_weight.reshape(4, 2, 16, D),
        query_gain, key_gain, gate_scale, neighbours, tile_slot[None],
    )
    return fwd[None], bwd.reshape(1, TILE, D), gate


def solution(mesh):
    in_specs = (
        P("pipe", ("dp", "seq"), None),
        P("pipe", ("dp", "seq"), None),
        P("pipe", None, "seq", None),
        P("pipe", "seq", None),
        P("pipe", None),
        P("pipe", None),
        P("pipe", None),
        P("dp", None),
        P("dp"),
    )
    out_specs = (
        P("pipe", ("dp", "seq"), None),
        P("pipe", ("dp", "seq"), None),
        P(("dp", "pipe"), "seq"),
    )
    return jax.shard_map(body, mesh=mesh, in_specs=in_specs, out_specs=out_specs, check_vma=False)
```

```python
import functools
import math

import jax
import jax.numpy as jnp
from jax import lax
from jax.experimental import pallas as pl
from jax.experimental.pallas import tpu as pltpu
from jax.sharding import PartitionSpec as P

EPSILON = 1e-06
MESH = pl.DeviceIdType.MESH
F32 = jnp.float32
BF16 = jnp.bfloat16
D = 3072
HD = 128
TILE = 64
NZ = 8
QB = 256
NQ = 4
COLS = 512
NT = (((1,), (1,)), ((), ()))


def dot(a, b):
    return jnp.dot(a, b, preferred_element_type=F32)


def dot_nt(a, b):
    return lax.dot_general(a, b, NT, preferred_element_type=F32)


def kernel(
    stream, upstream, wqkv, wout, qgain, kgain, gate, neigh, tslot,
    both_out, gate_out,
    Sg, UP, SC, WQ, WO, PJX, PJ1, BIAS, Qb, Kb, Vb, KT, VT, Pb, ATT, AH, DOS, DO,
    dQ, dK, dV, PG, PGX, WT, GT, SB, RB, AOUT, AOX, FO, BO, GS, GR,
    ld, zs_s, zs_r, zw_s, zw_r, xw_s, xw_r, pj_s, pj_r, ex_s, ex_r,
    at_s, at_r, do_s, do_r, pg_s, pg_r, rs_s, rs_r, y_s, y_r, g_s, g_r,
):
    seq = lax.axis_index("seq")
    x = lax.axis_index("dp")
    y = lax.axis_index("pipe")
    z = lax.div(seq, 2)
    c = lax.rem(seq, 2)

    def dev(d, e=0):
        return {"seq": 2 * lax.rem(z + d, NZ) + (c if e == 0 else 1 - c)}

    right, left, partner = dev(1), dev(NZ - 1), dev(0, 1)
    xr = {"dp": lax.rem(x + 1, 4)}
    xl = {"dp": lax.rem(x + 3, 4)}
    yn = {"pipe": lax.rem(y + 1, 4)}
    yp = {"pipe": lax.rem(y + 3, 4)}

    sent = []

    def remote(src, dst, ssem, rsem, to):
        return pltpu.make_async_remote_copy(
            src_ref=src, dst_ref=dst, send_sem=ssem, recv_sem=rsem,
            device_id=to, device_id_type=MESH)

    def go(copy):
        copy.start()
        sent.append(copy)

    loads = [
        pltpu.make_async_copy(wout, WO.at[0], ld.at[0]),
        pltpu.make_async_copy(stream, Sg.at[0], ld.at[1]),
        pltpu.make_async_copy(upstream, UP.at[0], ld.at[2]),
        pltpu.make_async_copy(wqkv, WQ.at[0], ld.at[3]),
    ]
    for copy in loads:
        copy.start()

    barrier = pltpu.get_barrier_semaphore()
    peers = [right, left, partner, xr, xl, yn, yp]
    for peer in peers:
        pl.semaphore_signal(barrier, inc=1, device_id=peer, device_id_type=MESH)
    pl.semaphore_wait(barrier, len(peers))

    def at(way, j):
        return (NZ - j) % NZ if way == 0 else j % NZ

    def ring_to(way):
        return right if way == 0 else left

    def s_unit(way, k):
        j, half = k // 2, (k + way) % 2
        return remote(Sg.at[at(way, j), half], Sg.at[at(way, j + 1), half],
                      zs_s.at[way, k], zs_r.at[way, k], ring_to(way))

    def w_unit(way, k):
        j, half = k // 2, (k + way) % 2
        return remote(WO.at[at(way, j), x, half], WO.at[at(way, j + 1), x, half],
                      zw_s.at[way, k], zw_r.at[way, k], ring_to(way))

    def x_unit(d, way, part):
        quarter = x if part < 2 else lax.rem(x + (3 if way == 0 else 1), 4)
        ref = WO.at[d, quarter, part if part < 2 else way]
        return remote(ref, ref, xw_s.at[d, way, part], xw_r.at[d, way, part], xr if way == 0 else xl)

    def s_wait(k):
        for way in (0, 1):
            s_unit(way, k).wait_recv()

    def s_next(k):
        s_wait(k)
        if k + 2 <= 6:
            for way in (0, 1):
                go(s_unit(way, k + 2))

    def w_next(k):
        for way in (0, 1):
            w_unit(way, k).wait_recv()
            if k + 2 <= 6:
                go(w_unit(way, k + 2))

    def x_send(d, half):
        for way in (0, 1):
            go(x_unit(d, way, half))

    def x_both(d):
        for half in (0, 1):
            for way in (0, 1):
                go(x_unit(d, way, (half + way) % 2))

    def x_next(d, way):
        x_unit(d, way, way).wait_recv()
        go(x_unit(d, way, 2))

    def x_done(d):
        for way in (0, 1):
            x_unit(d, way, 1 - way).wait_recv()
            x_unit(d, way, 2).wait_recv()

    def project(ds):
        rows = [Sg.at[d] for d in ds]

        def one(e, carry):
            lhs = [r[...].reshape(TILE, D) for r in rows]
            lhs = lhs[0] if len(lhs) == 1 else jnp.concatenate(lhs, axis=0)
            out = dot(lhs, WQ[e])
            for n, d in enumerate(ds):
                PJX[e, d] = out[n * TILE:(n + 1) * TILE]
            return carry

        lax.fori_loop(0, 2, one, 0)
        for d in ds:
            go(pj_unit(d))

    def pj_unit(d):
        return remote(PJX.at[1, d], PJ1.at[d], pj_s.at[d], pj_r.at[d], partner)

    def do_unit(d):
        return remote(DOS.at[d], DO.at[(NZ - d) % NZ], do_s.at[d], do_r.at[d], dev(d))

    def grads_in(ds):
        for d in ds:
            val = dot_nt(SC[...], WO[d].reshape(HD, D)).astype(BF16)
            if d == 0:
                DO[0] = val
            else:
                DOS[d] = val
                go(do_unit(d))

    up_x = remote(UP.at[0], UP.at[1], ex_s.at[0], ex_r.at[0], partner)
    wq_x = remote(WQ.at[0], WQ.at[1], ex_s.at[1], ex_r.at[1], partner)

    loads[0].wait()
    for k in (0, 1):
        for way in (0, 1):
            go(w_unit(way, k))
    loads[1].wait()
    loads[2].wait()
    go(up_x)
    loads[3].wait()
    go(wq_x)

    i_rows = lax.broadcasted_iota(jnp.int32, (16, 16), 0)
    rel_z = z + lax.div(i_rows, 2)
    rel_z = jnp.where(rel_z >= NZ, rel_z - NZ, rel_z)
    odd = lax.rem(i_rows, 2)
    rel_slot = 2 * rel_z + jnp.where(odd == 0, c, 1 - c)
    lanes16 = lax.broadcasted_iota(jnp.int32, (16, 16), 1)
    listed = jnp.zeros((16, 16), F32)
    for k in range(neigh.shape[1]):
        listed = listed + jnp.where(neigh[:, k:k + 1] == lanes16, 1.0, 0.0)
    holds = jnp.where(rel_slot == tslot[...], 1.0, 0.0)
    by_key = dot_nt(holds, listed)
    by_key = dot_nt(by_key, holds)
    spread = jnp.where(
        lax.div(lax.broadcasted_iota(jnp.int32, (16, 1024), 1), TILE)
        == lax.broadcasted_iota(jnp.int32, (16, 1024), 0), 1.0, 0.0)
    bias = jnp.where(dot(by_key, spread) > 0.5, 0.0, -jnp.inf)
    for n in range(NQ):
        BIAS[n] = bias[:, n * QB:(n + 1) * QB]

    def both(d):
        return jnp.concatenate([PJX[0, d], PJ1[d]], axis=0)

    def unit_of(part):
        spread = jnp.sqrt(jnp.mean(part * part, axis=-1, keepdims=True) + EPSILON)
        return part / spread, spread

    def norm(ds):
        for d in ds:
            pj_unit(d).wait_recv()
            pj = both(d)
            q_unit, _ = unit_of(pj[:, :HD])
            k_unit, _ = unit_of(pj[:, HD:2 * HD])
            Qb[d] = (q_unit * qgain[...]).astype(BF16)
            k = k_unit * kgain[...]
            v = pj[:, 2 * HD:]
            Kb[d] = k.astype(BF16)
            Vb[d] = v.astype(BF16)
            KT[:, d * HD:(d + 1) * HD] = k.T.astype(BF16)
            VT[:, d * HD:(d + 1) * HD] = v.T.astype(BF16)

    def flip(e):
        def one(n, carry):
            rows = pl.ds(pl.multiple_of(n * COLS, COLS), COLS)
            WT[e * 3 * HD:(e + 1) * 3 * HD, rows] = WQ[e, rows, :].T
            return carry

        lax.fori_loop(0, D // COLS, one, 0)

    w_next(0)
    x_send(7, 0)
    w_next(1)
    x_send(7, 1)
    for k in (0, 1):
        for way in (0, 1):
            go(s_unit(way, k))
    up_x.wait_recv()
    SC[...] = (UP[...].astype(F32) * gate[...]).astype(BF16).reshape(2 * TILE, D)
    x_next(7, 0)
    w_next(2)
    x_send(6, 0)
    x_send(2, 1)
    x_next(7, 1)
    w_next(3)
    x_send(6, 1)
    x_send(2, 0)
    wq_x.wait_recv()
    project([0])
    grads_in([0])
    x_next(6, 0)
    x_next(2, 1)
    s_next(0)
    x_done(7)
    grads_in([7])
    x_next(2, 0)
    x_next(6, 1)
    s_next(1)
    project([7, 1])
    w_next(4)
    x_send(5, 0)
    x_send(3, 1)
    w_next(5)
    x_send(5, 1)
    x_send(3, 0)
    flip(0)
    x_done(6)
    x_done(2)
    grads_in([6, 2])
    s_next(2)
    x_next(5, 0)
    x_next(3, 1)
    norm([0, 7, 1])
    x_next(3, 0)
    x_next(5, 1)
    s_next(3)
    project([6, 2])
    w_next(6)
    x_both(4)
    x_both(1)
    flip(1)
    x_done(5)
    x_done(3)
    grads_in([5, 3])
    s_next(4)
    norm([6, 2])
    x_next(4, 0)
    x_next(4, 1)
    s_next(5)
    project([5, 3])
    x_next(1, 0)
    x_next(1, 1)
    x_done(4)
    grads_in([4])
    norm([5, 3])
    s_next(6)
    project([4])
    norm([4])
    scale = 1.0 / math.sqrt(HD)

    def block(ref, n):
        return ref[pl.ds(2 * n, 2)].reshape(QB, HD)

    def attend(n, carry):
        s = dot_nt(Kb[...].reshape(NZ * HD, HD), block(Qb, n)) * (scale * math.log2(math.e))
        s = s.reshape(16, TILE, QB) + BIAS[n][:, None, :]
        s = s.reshape(NZ * HD, QB)
        p = jnp.exp2(s - jnp.max(s, axis=0, keepdims=True))
        p = (p * (1.0 / jnp.sum(p, axis=0, keepdims=True))).astype(BF16)
        Pb[n] = p
        ATT[pl.ds(2 * n, 2)] = dot(VT[...], p).T.astype(BF16).reshape(2, HD, HD)
        return carry

    lax.fori_loop(0, 2, attend, 0)
    x_done(1)
    grads_in([1])
    lax.fori_loop(2, NQ, attend, 0)

    def at_unit(d):
        back = (NZ - d) % NZ
        return remote(ATT.at[d], AH.at[:, back * HD:(back + 1) * HD], at_s.at[d], at_r.at[d], dev(d))

    for d in range(1, NZ):
        go(at_unit(d))
    AH[:, :HD] = ATT[0]
    dK[...] = jnp.zeros_like(dK)
    dV[...] = jnp.zeros_like(dV)
    for d in (7, 6, 5, 4, 3):
        do_unit(d).wait_recv()

    def attend_back(n, carry):
        grad, p = block(DO, n), Pb[n]
        dV[...] += dot(p, grad)
        dp = dot_nt(Vb[...].reshape(NZ * HD, HD), grad)
        wide = p.astype(F32)
        delta = jnp.sum(wide * dp, axis=0, keepdims=True)
        ds = (wide * (dp - delta) * scale).astype(BF16)
        dK[...] += dot(ds, block(Qb, n))
        dQ[pl.ds(2 * n, 2)] = dot(KT[...], ds).T.reshape(2, HD, HD)
        return carry

    lax.fori_loop(0, NQ - 1, attend_back, 0)
    for d in (2, 1):
        do_unit(d).wait_recv()
    attend_back(NQ - 1, 0)

    def norm_back(ds):
        for d in ds:
            pj = both(d)

            def one(part, grad, gain):
                unit, spread = unit_of(part)
                a = grad * gain
                return (a - unit * jnp.mean(a * unit, axis=-1, keepdims=True)) / spread

            gq = one(pj[:, :HD], dQ[d], qgain[...])
            gk = one(pj[:, HD:2 * HD], dK[d * HD:(d + 1) * HD, :], kgain[...])
            pg = jnp.concatenate([gq, gk, dV[d * HD:(d + 1) * HD, :]], axis=1).astype(BF16)
            PG[d, :, :3 * HD] = pg[:TILE]
            PGX[d] = pg[TILE:]
            go(pg_unit(d))

    def pg_unit(d):
        return remote(PGX.at[d], PG.at[d, :, 3 * HD:], pg_s.at[d], pg_r.at[d], partner)

    norm_back([4, 3, 5])

    def group(ds):
        for d in ds:
            pg_unit(d).wait_recv()

        def one(n, carry):
            cols = pl.ds(pl.multiple_of(n * COLS, COLS), COLS)
            rows = jnp.concatenate([PG[d] for d in ds], axis=0)
            out = dot(rows, WT[:, cols])
            for i, d in enumerate(ds):
                GT[d, :, cols] = out[i * TILE:(i + 1) * TILE]
            return carry

        lax.fori_loop(0, D // COLS, one, 0)

    ends = [(1, 2), (1, 3), (1, 0), (1, 1)]
    plan = [
        [(4, 0), (4, 1), (3, 2), (3, 3), (3, 0), (3, 1), (2, 2), (2, 3), (2, 0), (2, 1)] + ends,
        [(4, 2), (4, 3), (3, 0), (3, 1), (3, 2), (3, 3), (2, 0), (2, 1), (2, 2), (2, 3)] + ends,
    ]

    def rs_unit(way, k):
        return remote(SB.at[way, k], RB.at[way, k], rs_s.at[way, k], rs_r.at[way, k], ring_to(way))

    def rs_send(k):
        for way in (0, 1):
            dist, q = plan[way][k]
            val = GT[dist if way == 0 else NZ - dist, q * 16:(q + 1) * 16, :]
            if (dist + 1, q) in plan[way]:
                needs = plan[way].index((dist + 1, q))
                rs_unit(way, needs).wait_recv()
                val = val + RB[way, needs].astype(F32)
            SB[way, k] = val.astype(BF16)
            go(rs_unit(way, k))

    group([4, 3, 5])
    rs_send(0)
    rs_send(1)
    rs_send(2)
    rs_send(3)
    norm_back([2, 6])
    rs_send(4)
    norm_back([1, 7])
    rs_send(5)
    group([2, 6])
    rs_send(6)
    rs_send(7)
    norm_back([0])
    rs_send(8)
    group([1, 7, 0])
    rs_send(9)

    for d in range(1, NZ):
        at_unit(d).wait_recv()

    def out_proj(n, carry):
        cols = pl.ds(pl.multiple_of(n * COLS, COLS), COLS)
        w = WO[:, :, :, :, cols].reshape(NZ * HD, COLS)
        out = dot(AH[...], w)
        AOUT[0, :, cols] = out[:TILE]
        AOUT[1, :, cols] = out[TILE:]
        return carry

    lax.fori_loop(0, D // COLS, out_proj, 0)
    ao_x = remote(AOUT.at[1], AOX, ex_s.at[3], ex_r.at[3], partner)
    go(ao_x)
    rs_send(10)
    rs_send(11)
    rs_send(12)
    rs_send(13)
    ao_x.wait_recv()
    wide_ao = AOUT[0] + AOX[...]
    FO[...] = (Sg[0].reshape(TILE, D).astype(F32) + gate[...] * wide_ao).astype(BF16)
    fo_y = remote(FO, both_out.at[0], y_s.at[0], y_r.at[0], yn)
    go(fo_y)
    gsum = jnp.sum((UP[0].astype(F32) * wide_ao).reshape(8, 8, D), axis=0)
    for n in range(16):
        GS[n] = gsum[:, n * 192:(n + 1) * 192]

    def g_unit(d, e):
        i = 2 * d + e
        own = dev(d, e)["seq"]
        return remote(GS.at[own], GR.at[2 * ((NZ - d) % NZ) + e], g_s.at[i], g_r.at[i], dev(d, e))

    pairs = [(d, e) for d in range(NZ) for e in range(2) if d or e]
    for d, e in pairs:
        go(g_unit(d, e))
    GR[0] = GS[seq]

    def bo_unit(q):
        return remote(BO.at[q], both_out.at[1, q * 16:(q + 1) * 16], y_s.at[1 + q], y_r.at[1 + q], yp)

    for dist, q in ends:
        total = GT[0, q * 16:(q + 1) * 16, :]
        for way in (0, 1):
            k = plan[way].index((dist, q))
            rs_unit(way, k).wait_recv()
            total = total + RB[way, k].astype(F32)
        BO[q] = (UP[0, q * 16:(q + 1) * 16, :].astype(F32) + total).astype(BF16)
        go(bo_unit(q))

    for d, e in pairs:
        g_unit(d, e).wait_recv()
    gate_out[...] = jnp.sum(jnp.sum(GR[...], axis=0), axis=0, keepdims=True)
    fo_y.wait_recv()
    for q in range(4):
        bo_unit(q).wait_recv()
    for copy in sent:
        copy.wait_send()


def body(segment_input, output_grad, qkv_weight, out_weight, query_gain, key_gain, gate_scale,
         neighbours, tile_slot):
    dma = pltpu.SemaphoreType.DMA
    vm = pltpu.VMEM
    scratch = [
        vm((NZ, 2, 32, D), BF16),
        vm((2, TILE, D), BF16),
        vm((2 * TILE, D), BF16),
        vm((2, D, 3 * HD), BF16),
        vm((NZ, 4, 2, 16, D), BF16),
        vm((2, NZ, TILE, 3 * HD), F32),
        vm((NZ, TILE, 3 * HD), F32),
        vm((NQ, 16, QB), F32),
        vm((NZ, HD, HD), BF16),
        vm((NZ, HD, HD), BF16),
        vm((NZ, HD, HD), BF16),
        vm((HD, NZ * HD), BF16),
        vm((HD, NZ * HD), BF16),
        vm((NQ, NZ * HD, QB), BF16),
        vm((NZ, HD, HD), BF16),
        vm((HD, NZ * HD), BF16),
        vm((NZ, HD, HD), BF16),
        vm((NZ, HD, HD), BF16),
        vm((NZ, HD, HD), F32),
        vm((NZ * HD, HD), F32),
        vm((NZ * HD, HD), F32),
        vm((NZ, TILE, 6 * HD), BF16),
        vm((NZ, TILE, 3 * HD), BF16),
        vm((6 * HD, D), BF16),
        vm((NZ, TILE, D), F32),
        vm((2, 14, 16, D), BF16),
        vm((2, 14, 16, D), BF16),
        vm((2, TILE, D), F32),
        vm((TILE, D), F32),
        vm((TILE, D), BF16),
        vm((4, 16, D), BF16),
        vm((16, 8, 192), F32),
        vm((16, 8, 192), F32),
        dma((4,)), dma((2, 7)), dma((2, 7)), dma((2, 7)), dma((2, 7)), dma((NZ, 2, 3)), dma((NZ, 2, 3)),
        dma((NZ,)), dma((NZ,)), dma((4,)), dma((4,)), dma((NZ,)), dma((NZ,)), dma((NZ,)), dma((NZ,)),
        dma((NZ,)), dma((NZ,)), dma((2, 14)), dma((2, 14)), dma((5,)), dma((5,)), dma((16,)), dma((16,)),
    ]
    any_spec = pl.BlockSpec(memory_space=pl.ANY)
    vm_spec = pl.BlockSpec(memory_space=pltpu.VMEM)
    out, gate = pl.pallas_call(
        kernel,
        name="section",
        out_shape=(
            jax.ShapeDtypeStruct((2, TILE, D), BF16),
            jax.ShapeDtypeStruct((1, 192), F32),
        ),
        in_specs=[any_spec] * 4 + [vm_spec] * 5,
        out_specs=(any_spec, vm_spec),
        scratch_shapes=scratch,
        compiler_params=pltpu.CompilerParams(
            collective_id=0, has_side_effects=True, vmem_limit_bytes=56 * 1024 * 1024),
    )(
        segment_input.reshape(2, 32, D),
        output_grad.reshape(TILE, D),
        qkv_weight.reshape(D, 3 * HD),
        out_weight.reshape(4, 2, 16, D),
        query_gain, key_gain, gate_scale, neighbours, tile_slot[None],
    )
    return out[:1], out[1:], gate


def solution(mesh):
    in_specs = (
        P("pipe", ("dp", "seq"), None),
        P("pipe", ("dp", "seq"), None),
        P("pipe", None, "seq", None),
        P("pipe", "seq", None),
        P("pipe", None),
        P("pipe", None),
        P("pipe", None),
        P("dp", None),
        P("dp"),
    )
    out_specs = (
        P("pipe", ("dp", "seq"), None),
        P("pipe", ("dp", "seq"), None),
        P(("dp", "pipe"), "seq"),
    )
    return jax.shard_map(body, mesh=mesh, in_specs=in_specs, out_specs=out_specs, check_vma=False)
```
